256 devices in a mesh: dp: 8 (over z), label: 16 (over x, y), section: 2 (over core).
Axes of the slice: x: 4, y: 4, z: 8, core: 2. Of those that a mesh axis runs over, the one named last changes fastest.
Arguments:
- queries: bfloat16 [32768, 1024], P(('dp', 'label', 'section')), may hold values from -6 to 6
- label_weights: bfloat16 [128, 128, 1024], P('label'), may hold values from -0.1875 to 0.1875
- propensity: float32 [128, 128], P('label'), may hold values from 0.1 to 1
- positives: int32 [32768, 8], P(('dp', 'label', 'section')), may hold values from 0 to 6143
- shortlist: int32 [128, 48], P(('dp', 'label')), may hold values from 0 to 127, as said below
- owner_map: int32 [128], replicated, may hold values from 0 to 127, as said below
Outputs:
- query_grad: float32 [32768, 1024], P(('dp', 'label', 'section'))
- weight_grad: float32 [128, 128, 1024], P('label', ('dp', 'section'))
The draws below stay inside these ranges and needn't reach their ends.
Inputs may be any that keep to these rules, and one draw needn't show every extreme that they name: owner_map is a permutation of the 128 row blocks. `shortlist`: each row lists 48 different label-block ids. Of one row's blocks at most 6 are stored in the row blocks of one owner (rows o * 8 to o * 8 + 7 of label_weights), and in every draw one owner holds exactly 6 of the blocks of every row.
All inputs are finite; a program needn't handle non-finite values.
Results may differ from the reference program's by a relative error of at most 0.0021.
Values may be sent and summed in bfloat16 or wider, within the bound.
A program may use at most 128 MiB of HBM per device.

```python
import math
import jax
import jax.numpy as jnp
from jax import lax

D = 1024
LB = 128
QR = 256
SHORT = 48
POS = 8
CAP = 6
BLK_DEV = 8
NBLK = 128
Q_BLOCKS = 128
QUERIES = 32768
N_LABEL = 16


def ownership_perm(key):
    return jax.random.permutation(jax.random.fold_in(key, 11), NBLK).astype(jnp.int32)


def draw_owner_map(key, part):
    return ownership_perm(key)


def draw_shortlist(key, part):
    storage_perm = ownership_perm(key)
    inverse = jnp.argsort(storage_perm, stable=True).astype(jnp.int32)
    hot_owner = jax.random.randint(jax.random.fold_in(key, 12), (), 0, N_LABEL).astype(jnp.int32)
    hot_slots = (jax.random.randint(jax.random.fold_in(key, 13), (N_LABEL, BLK_DEV), 0, 4) == 0).astype(jnp.int32)
    spread = (SHORT - CAP + N_LABEL - 2) // (N_LABEL - 1)
    row_keys = jax.random.split(jax.random.fold_in(key, 14), Q_BLOCKS)

    def one_row(row_key):
        key_owner = jax.random.fold_in(row_key, 1)
        key_slot = jax.random.fold_in(row_key, 2)
        key_shuffle = jax.random.fold_in(row_key, 3)
        places = jax.random.permutation(key_owner, (N_LABEL - 1) * spread)[:SHORT - CAP].astype(jnp.int32)
        others = places // spread
        other_count = jnp.sum((others[:, None] == jnp.arange(N_LABEL - 1, dtype=jnp.int32)[None, :]).astype(jnp.int32), axis=0)
        owner_idx = jnp.arange(N_LABEL, dtype=jnp.int32)
        shifted = jnp.clip(owner_idx - (owner_idx > hot_owner).astype(jnp.int32), 0, N_LABEL - 2)
        counts = jnp.where(owner_idx == hot_owner, CAP, other_count[shifted])
        jitter = jax.random.randint(key_slot, (N_LABEL, BLK_DEV), 0, 65536).astype(jnp.int32)
        ranking = (jitter + hot_slots * 65536) * BLK_DEV + jnp.arange(BLK_DEV, dtype=jnp.int32)[None, :]
        picked = lax.top_k(ranking, CAP)[1].astype(jnp.int32)
        stored = owner_idx[:, None] * BLK_DEV + picked
        live_mask = (jnp.arange(CAP, dtype=jnp.int32)[None, :] < counts[:, None]).astype(jnp.int32)
        keep_order = jnp.argsort(1 - live_mask.reshape(-1), stable=True)[:SHORT]
        chosen = stored.reshape(-1)[keep_order]
        chosen = chosen[jax.random.permutation(key_shuffle, SHORT)]
        return inverse[chosen]
    return jax.vmap(one_row)(row_keys).astype(jnp.int32)


def with_ends(drawn, stream_key, low, largest):
    place = [jax.random.randint(jax.random.fold_in(stream_key, axis), (), 0, length) for axis, length in enumerate(drawn.shape)]
    main_axis = drawn.shape.index(max(drawn.shape))
    beside = place[:main_axis] + [(place[main_axis] + 1) % drawn.shape[main_axis]] + place[main_axis + 1:]
    return drawn.at[tuple(place)].set(low).at[tuple(beside)].set(largest)


def levels(stream_key, extent, cuts, low, largest):
    loudness, own = 1.0, jax.random.fold_in(stream_key, 6)
    for position, parts in cuts:
        heights = jnp.exp(jax.random.uniform(jax.random.fold_in(own, position), (parts,), jnp.float32, low / len(cuts), largest / len(cuts)))
        loudness = loudness * jnp.repeat(heights, extent[position] // parts).reshape([-1 if axis == position else 1 for axis in range(len(extent))])
    return loudness


def gaussian(rng, shape, deviation, most, shards=(), kind=jnp.bfloat16):
    level = levels(rng, shape, shards, -0.22, 0.18) if shards else 1.0
    drawn = jax.random.normal(rng, shape, jnp.float32) * deviation * level
    return jnp.minimum(jnp.maximum(drawn, -most), most).astype(kind)


def setup_inputs(seed: int = 0) -> dict:
    splits = jax.random.split(jax.random.key(seed), 7)
    return {
        "queries": gaussian(splits[0], (QUERIES, D), 1.0, 6.0, ((0, 256),)),
        "label_weights": gaussian(splits[1], (NBLK, LB, D), D ** -0.5, 0.1875, ((0, 16),)),
        "propensity": jnp.clip(jnp.exp(math.log(1.0) - 2.3025851 * jax.random.uniform(splits[2], (NBLK, LB), jnp.float32) ** levels(splits[2], (NBLK, LB), ((0, 16),), -0.2, 0.2)), 0.1, 1.0),
        "positives": with_ends(jax.random.randint(splits[3], (QUERIES, POS), 0, SHORT * LB), jax.random.fold_in(splits[3], 1), 0, (SHORT * LB) - 1).astype(jnp.int32),
        "shortlist": draw_shortlist(jax.random.fold_in(splits[6], 71), 0),
        "owner_map": draw_owner_map(jax.random.fold_in(splits[6], 71), 0),
    }


grad_scale = 0.25


def reference(queries, label_weights, propensity, positives, shortlist, owner_map):
    query_blocks = shortlist.shape[0]
    block_feats = queries.reshape(query_blocks, QR, D)
    pos_rows = positives.reshape(query_blocks, QR, POS)
    label_pos = jnp.arange(SHORT, dtype=jnp.int32)[:, None] * LB + jnp.arange(LB, dtype=jnp.int32)[None, :]
    highest = lax.Precision.HIGHEST

    def block_step(carry, inputs):
        block_rows, block_pos, block_list = inputs
        stored = owner_map[block_list].astype(jnp.int32)
        chosen = label_weights[stored].astype(jnp.float32)
        prop_sel = propensity[stored]
        features = block_rows.astype(jnp.float32)
        scores = jnp.einsum('qd,eld->eql', features, chosen, precision=highest)
        target = jnp.any(block_pos[None, :, :, None] == label_pos[:, None, None, :], axis=2).astype(jnp.float32)
        score_grad = (grad_scale * (jax.nn.sigmoid(scores) - target / prop_sel[:, None, :])).astype(jnp.bfloat16)
        grad_wide = score_grad.astype(jnp.float32)
        query_part = jnp.einsum('eql,eld->qd', grad_wide, chosen, precision=highest)
        weight_part = jnp.einsum('eql,qd->eld', grad_wide, features, precision=highest)
        carry = carry.at[stored].add(weight_part)
        return carry, query_part

    start_grad = jnp.zeros(label_weights.shape, jnp.float32)
    weight_grad, query_parts = lax.scan(block_step, start_grad, (block_feats, pos_rows, shortlist))
    return query_parts.reshape(query_blocks * QR, D), weight_grad
```

```python
import functools

import jax
import jax.numpy as jnp
from jax import lax
from jax.experimental import pallas as pl
from jax.experimental.pallas import tpu as pltpu
from jax.sharding import PartitionSpec as P

MESH = pl.DeviceIdType.MESH
SIDE = 4
RING = 8
HALF = 64
QUART = 32
grad_scale = 0.25
F32, BF16 = jnp.float32, jnp.bfloat16


def kernel(
    q_ref, w_ref, invp_ref, meta_ref, qg_ref, wo_ref,
    q_all, part, wg, sg, meta_all, pos_t, labid,
    s1s, s1r, s2r, xr, zr,
    ag_ss, ag_rs, me_ss, me_rs, s1_ss, s1_rs, s2_ss, s2_rs, x_ss, x_rs, z_ss, z_rs, loc_s,
):
    label = lax.axis_index("label")
    z = lax.axis_index("dp")
    core = lax.axis_index("section")
    x, y = label // SIDE, label % SIDE

    def at(dx, dy):
        return {"label": lax.rem(x + dx + SIDE, SIDE) * SIDE + lax.rem(y + dy + SIDE, SIDE)}

    def along(axis, d):
        return at(d, 0) if axis == 0 else at(0, d)

    def slow(c, d):
        return along(c, d)

    def fast(c, d):
        return along(1 - c, d)

    def zdev(d):
        return {"dp": lax.rem(z + d + RING, RING)}

    other = {"section": 1 - core}

    peers = [at(d, 0) for d in (1, 2, 3)] + [at(0, d) for d in (1, 2, 3)] + [zdev(1), zdev(-1), other]
    barrier = pltpu.get_barrier_semaphore()
    for peer in peers:
        pl.semaphore_signal(barrier, inc=1, device_id=peer, device_id_type=MESH)
    pl.semaphore_wait(barrier, len(peers))

    def remote(src, dst, ss, rs, dev):
        return pltpu.make_async_remote_copy(
            src_ref=src, dst_ref=dst, send_sem=ss, recv_sem=rs, device_id=dev, device_id_type=MESH
        )

    started = []

    def go(copy):
        copy.start()
        started.append(copy)
        return copy

    lo, hi = pl.ds(0, QUART), pl.ds(QUART, QUART)
    ag = {}

    def ag_send(c, slot, kind, src, dst, dev):
        ag[c, slot, kind] = go(remote(src, dst, ag_ss.at[c, slot, kind], ag_rs.at[c, slot, kind], dev))

    def p1a(c):
        ag_send(c, 4, 0, q_ref.at[c], q_all.at[0, c, 3], slow(c, 1))
        ag_send(c, 4, 1, q_ref.at[c], q_all.at[0, c, 1], slow(c, -1))

    def p1b(c, kind):
        ag[c, 4, kind].wait_recv()
        if kind == 0:
            ag_send(c, 4, 2, q_all.at[0, c, 3, lo], q_all.at[0, c, 2, lo], slow(c, 1))
        else:
            ag_send(c, 4, 3, q_all.at[0, c, 1, hi], q_all.at[0, c, 2, hi], slow(c, -1))

    def p2a(c, j):
        src = q_ref.at[c] if j == 0 else q_all.at[0, c, j]
        ag_send(c, j, 0, src, q_all.at[3, c, j], fast(c, 1))
        ag_send(c, j, 1, src, q_all.at[1, c, j], fast(c, -1))

    def p2b(c, j):
        ag[c, j, 0].wait_recv()
        ag_send(c, j, 2, q_all.at[3, c, j, lo], q_all.at[2, c, j, lo], fast(c, 1))
        ag[c, j, 1].wait_recv()
        ag_send(c, j, 3, q_all.at[1, c, j, hi], q_all.at[2, c, j, hi], fast(c, -1))

    p1a(0)
    p1a(1)
    locals_ = [
        pltpu.make_async_copy(meta_ref, meta_all.at[0, 0], loc_s.at[0]),
        pltpu.make_async_copy(q_ref.at[0], q_all.at[0, 0, 0], loc_s.at[1]),
        pltpu.make_async_copy(q_ref.at[1], q_all.at[0, 1, 0], loc_s.at[2]),
    ]
    for copy in locals_:
        copy.start()
    meta_x = [
        go(remote(meta_ref, meta_all.at[SIDE - a, 0], me_ss.at[0, a], me_rs.at[0, a], at(a, 0)))
        for a in (1, 2, 3)
    ]
    p2a(0, 0)
    p2a(1, 0)
    for copy in locals_:
        copy.wait()
    wg[...] = jnp.zeros_like(wg)
    for copy in meta_x:
        copy.wait_recv()
    meta_y = [
        go(remote(meta_all.at[:, 0], meta_all.at[:, SIDE - a], me_ss.at[1, a], me_rs.at[1, a], at(0, a)))
        for a in (1, 2, 3)
    ]
    for c in (0, 1):
        p1b(c, 0)
        p1b(c, 1)
    for c in (0, 1):
        p2a(c, 3)
        p2a(c, 1)
    for copy in meta_y:
        copy.wait_recv()

    def prepare(d, carry):
        dx, dy = d // SIDE, d % SIDE
        tile = meta_all[dx, dy]
        pos_t[d] = jnp.transpose(tile[0:8, :])
        lane = lax.broadcasted_iota(jnp.int32, (8, 128), 1)
        sub = lax.broadcasted_iota(jnp.int32, (8, 128), 0)
        entry = jnp.sum(
            jnp.where(lane == label * 8 + sub, jnp.broadcast_to(tile[8:9, :], (8, 128)), 0),
            axis=1, keepdims=True,
        )
        labid[d] = jnp.where(entry >= 0, entry * 128 + lane, -1)
        return carry

    lax.fori_loop(0, SIDE * SIDE, prepare, 0)
    for c in (0, 1):
        ag[c, 4, 2].wait_recv()
        ag[c, 4, 3].wait_recv()
        p2a(c, 2)
    for c in (0, 1):
        p2b(c, 0)

    def score_chunk(k):
        def body(n, carry):
            rows = q_all[k].reshape(2 * SIDE * HALF, 1024)
            s = lax.dot_general(
                rows, w_ref[pl.ds(pl.multiple_of(n * 256, 256), 256), :],
                (((1,), (1,)), ((), ())), preferred_element_type=F32,
            )
            for c in (0, 1):
                for j in range(SIDE):
                    dev = j * SIDE + k if c == 0 else k * SIDE + j
                    r0 = (c * SIDE + j) * HALF
                    pos = pos_t[dev, c * HALF : (c + 1) * HALF, :]
                    cols = [jnp.broadcast_to(pos[:, p : p + 1], (HALF, 128)) for p in range(8)]
                    for b in (0, 1):
                        ids = labid[dev, pl.ds(2 * n + b, 1), :]
                        inv = invp_ref[pl.ds(2 * n + b, 1), :]
                        hit = cols[0] == ids
                        for p in range(1, 8):
                            hit = hit | (cols[p] == ids)
                        sig = jax.nn.sigmoid(s[r0 : r0 + HALF, b * 128 : (b + 1) * 128])
                        g = (sig - jnp.where(hit, inv, 0.0)) * jnp.where(ids >= 0, grad_scale, 0.0)
                        sg[r0 : r0 + HALF, pl.ds(pl.multiple_of(n * 256 + b * 128, 128), 128)] = g.astype(BF16)
            return carry

        lax.fori_loop(0, 4, body, 0)

    def query_chunk(k):
        def body(n, carry):
            cols = pl.ds(pl.multiple_of(n * 256, 256), 256)
            part[k, :, :, :, cols] = jnp.dot(
                sg[...], w_ref[:, cols], preferred_element_type=F32
            ).reshape(2, SIDE, HALF, 256)
            return carry

        lax.fori_loop(0, 4, body, 0)

    def weight_chunk(k):
        def body(n, carry):
            cols = pl.ds(pl.multiple_of(n * 256, 256), 256)
            out = lax.dot_general(
                sg[:, cols], q_all[k].reshape(2 * SIDE * HALF, 1024),
                (((0,), (0,)), ((), ())), preferred_element_type=F32,
            )
            rows = pl.ds(n * 2, 2)
            wg[rows] = wg[rows] + out.reshape(2, 16, 8, 1024)
            return carry

        lax.fori_loop(0, 4, body, 0)

    s1 = {}

    def s1_send(c, d, m, k, half):
        def body(j, carry):
            s1s[c, d, m, j] = part[k, c, j, half * QUART : (half + 1) * QUART, :].astype(BF16)
            return carry

        lax.fori_loop(0, SIDE, body, 0)
        s1[c, d, m] = go(
            remote(s1s.at[c, d, m], s1r.at[c, d, m], s1_ss.at[c, d, m], s1_rs.at[c, d, m], fast(c, 1 - 2 * d))
        )

    def s1_add(c, d, m, k, half):
        s1[c, d, m].wait_recv()

        def body(j, carry):
            rows = slice(half * QUART, (half + 1) * QUART)
            part[k, c, j, rows, :] = part[k, c, j, rows, :] + s1r[c, d, m, j].astype(F32)
            return carry

        lax.fori_loop(0, SIDE, body, 0)

    score_chunk(0)
    for c in (0, 1):
        p2b(c, 3)
    query_chunk(0)
    for c in (0, 1):
        p2b(c, 1)
    weight_chunk(0)
    for c in (0, 1):
        p2b(c, 2)
    score_chunk(3)
    query_chunk(3)
    for c in (0, 1):
        s1_send(c, 1, 1, 3, 0)
    weight_chunk(3)
    score_chunk(1)
    query_chunk(1)
    for c in (0, 1):
        s1_send(c, 0, 1, 1, 1)
    weight_chunk(1)
    for c in (0, 1):
        for j in range(SIDE):
            ag[c, j, 2].wait_recv()
            ag[c, j, 3].wait_recv()
    score_chunk(2)
    query_chunk(2)
    for c in (0, 1):
        s1_send(c, 0, 0, 2, 0)
        s1_send(c, 1, 0, 2, 1)
    weight_chunk(2)

    def piece(r, own):
        return lax.rem(z + r, RING) * 2 + (core if own else 1 - core)

    order = (4, 3, 5, 2, 6, 1, 7, 0)
    ex = {
        r: go(remote(wg.at[:, piece(r, False)], xr.at[r], x_ss.at[r], x_rs.at[r], other)) for r in order
    }

    def ex_add(r):
        ex[r].wait_recv()
        i = piece(r, True)
        wg[:, i] = wg[:, i] + xr[r]

    zc = {}

    def z_send(d, t, h):
        r = 4 - t if d == 0 else 4 + t
        zc[d, t, h] = go(
            remote(
                wg.at[pl.ds(4 * h, 4), piece(r, True)], zr.at[d, t, h],
                z_ss.at[d, t, h], z_rs.at[d, t, h], zdev(1 - 2 * d),
            )
        )

    def z_add(d, t, h):
        zc[d, t, h].wait_recv()
        r = 3 - t if d == 0 else (5 + t) % RING
        i = piece(r, True)
        rows = slice(4 * h, 4 * h + 4)
        wg[rows, i] = wg[rows, i] + zr[d, t, h]

    s2 = {}

    def s2_send(c, d, m, j, half):
        s2[c, d, m] = go(
            remote(
                part.at[0, c, j, pl.ds(half * QUART, QUART)], s2r.at[c, d, m],
                s2_ss.at[c, d, m], s2_rs.at[c, d, m], slow(c, 1 - 2 * d),
            )
        )

    def s2_add(c, d, m, j, half):
        s2[c, d, m].wait_recv()
        rows = slice(half * QUART, (half + 1) * QUART)
        part[0, c, j, rows, :] = part[0, c, j, rows, :] + s2r[c, d, m]

    for c in (0, 1):
        s1_add(c, 1, 1, 0, 0)
        s1_add(c, 0, 1, 0, 1)
    for c in (0, 1):
        s1_add(c, 0, 0, 1, 0)
        s1_send(c, 0, 2, 1, 0)
        s1_add(c, 1, 0, 3, 1)
        s1_send(c, 1, 2, 3, 1)
    for r in (4, 3, 5):
        ex_add(r)
    z_send(0, 0, 0)
    z_send(1, 0, 1)
    z_send(0, 1, 1)
    z_send(1, 1, 0)
    for r in (2, 6, 1, 7, 0):
        ex_add(r)
    z_add(0, 0, 0)
    z_send(0, 1, 0)
    z_add(1, 0, 1)
    z_send(1, 1, 1)
    for c in (0, 1):
        s1_add(c, 0, 2, 0, 0)
        s1_add(c, 1, 2, 0, 1)
        s2_send(c, 0, 0, 2, 0)
        s2_send(c, 1, 0, 2, 1)
        s2_send(c, 0, 1, 1, 1)
        s2_send(c, 1, 1, 3, 0)
    for d, h in ((0, 1), (1, 0), (0, 0), (1, 1)):
        z_add(d, 1, h)
        z_send(d, 2, h)
    for c in (0, 1):
        s2_add(c, 0, 0, 1, 0)
        s2_send(c, 0, 2, 1, 0)
        s2_add(c, 1, 0, 3, 1)
        s2_send(c, 1, 2, 3, 1)
    for d, h in ((0, 1), (1, 0), (0, 0), (1, 1)):
        z_add(d, 2, h)
        z_send(d, 3, h)
    for c in (0, 1):
        s2_add(c, 0, 1, 0, 1)
        s2_add(c, 1, 1, 0, 0)
    for c in (0, 1):
        s2_add(c, 0, 2, 0, 0)
        s2_add(c, 1, 2, 0, 1)
        qg_ref[c] = part[0, c, 0]
    for d, h in ((0, 1), (1, 0), (0, 0), (1, 1)):
        z_add(d, 3, h)
    wo_ref[...] = wg[:, piece(0, True)]
    for copy in started:
        copy.wait_send()


def per_device(queries, label_weights, propensity, positives, shortlist, owner_map):
    blocks, block_rows, dim = label_weights.shape
    table = owner_map.shape[0]
    entries = jnp.arange(shortlist.shape[1], dtype=jnp.int32)
    ids = jnp.arange(table, dtype=jnp.int32)
    lookup = shortlist[0][:, None] == ids[None, :]
    stored = jnp.sum(jnp.where(lookup, owner_map[None, :], 0), axis=1)
    entry_of = jnp.sum(jnp.where(stored[:, None] == ids[None, :], entries[:, None] + 1, 0), axis=0) - 1
    meta = jnp.concatenate(
        [positives.T, entry_of[None, :], jnp.zeros((7, table), jnp.int32)], axis=0
    )
    vm = pl.BlockSpec(memory_space=pltpu.VMEM)
    dma = pltpu.SemaphoreType.DMA
    qg, wo = pl.pallas_call(
        kernel,
        out_shape=(
            jax.ShapeDtypeStruct((2, HALF, dim), F32),
            jax.ShapeDtypeStruct((blocks, 8, dim), F32),
        ),
        in_specs=[vm] * 4,
        out_specs=(vm, vm),
        scratch_shapes=[
            pltpu.VMEM((SIDE, 2, SIDE, HALF, dim), BF16),
            pltpu.VMEM((SIDE, 2, SIDE, HALF, dim), F32),
            pltpu.VMEM((blocks, 16, 8, dim), F32),
            pltpu.VMEM((2 * SIDE * HALF, blocks * block_rows), BF16),
            pltpu.VMEM((SIDE, SIDE, 16, 128), jnp.int32),
            pltpu.VMEM((SIDE * SIDE, 128, 8), jnp.int32),
            pltpu.VMEM((SIDE * SIDE, 8, 128), jnp.int32),
            pltpu.VMEM((2, 2, 3, SIDE, QUART, dim), BF16),
            pltpu.VMEM((2, 2, 3, SIDE, QUART, dim), BF16),
            pltpu.VMEM((2, 2, 3, QUART, dim), F32),
            pltpu.VMEM((RING, blocks, 8, dim), F32),
            pltpu.VMEM((2, 4, 2, 4, 8, dim), F32),
            dma((2, 5, 4)), dma((2, 5, 4)),
            dma((2, 4)), dma((2, 4)),
            dma((2, 2, 3)), dma((2, 2, 3)),
            dma((2, 2, 3)), dma((2, 2, 3)),
            dma((RING,)), dma((RING,)),
            dma((2, 4, 2)), dma((2, 4, 2)),
            dma((3,)),
        ],
        compiler_params=pltpu.CompilerParams(
            collective_id=0, has_side_effects=True, vmem_limit_bytes=60 * 1024 * 1024
        ),
    )(
        queries.reshape(2, HALF, dim),
        label_weights.reshape(blocks * block_rows, dim),
        1.0 / propensity,
        meta,
    )
    return qg.reshape(2 * HALF, dim), wo


def solution(mesh):
    in_specs = (
        P(("dp", "label", "section"), None),
        P("label", None, None),
        P("label", None),
        P(("dp", "label", "section"), None),
        P(("dp", "label"), None),
        P(),
    )
    out_specs = (P(("dp", "label", "section"), None), P("label", ("dp", "section"), None))
    return jax.shard_map(
        per_device, mesh=mesh, in_specs=in_specs, out_specs=out_specs, check_vma=False
    )
```

```python
import jax
import jax.numpy as jnp
from jax import lax
from jax.experimental import pallas as pl
from jax.experimental.pallas import tpu as pltpu
from jax.sharding import PartitionSpec as P

MESH = pl.DeviceIdType.MESH
SIDE = 4
RING = 8
HALF = 64
QUART = 32
TILES = 4
WIDE = 256
FAR = 1 << 20
grad_scale = 0.25
F32, BF16, I32 = jnp.float32, jnp.bfloat16, jnp.int32


def kernel(
    q_hbm, w_hbm, prop_hbm, pos_hbm, list_hbm, map_hbm, qg_ref, wo_ref,
    q_all, w_ref, prop_ref, list_ref, map_ref, meta, meta_all, words_t, live, inv,
    sg, p0, p1, p3, wg, s1s, s1r, s2s, s2r, s3s, s3r, xr, zs, zr, zfs, zfr,
    loc_s, me_ss, me_rs, ag_ss, ag_rs, s1_ss, s1_rs, s2_ss, s2_rs, x_ss, x_rs, z_ss, z_rs,
):
    label = lax.axis_index("label")
    z = lax.axis_index("dp")
    core = lax.axis_index("section")
    x, y = label // SIDE, label % SIDE
    rows_all = 2 * SIDE * HALF
    dim = SIDE * WIDE

    def at(dx, dy):
        return {"label": lax.rem(x + dx + SIDE, SIDE) * SIDE + lax.rem(y + dy + SIDE, SIDE)}

    def along(axis, d):
        return at(d, 0) if axis == 0 else at(0, d)

    def slow(c, d):
        return along(c, d)

    def fast(c, d):
        return along(1 - c, d)

    def zdev(d):
        return {"dp": lax.rem(z + d + RING, RING)}

    other = {"section": 1 - core}

    peers = [at(d, 0) for d in (1, 2, 3)] + [at(0, d) for d in (1, 2, 3)] + [zdev(1), zdev(-1), other]
    barrier = pltpu.get_barrier_semaphore()
    for peer in peers:
        pl.semaphore_signal(barrier, inc=1, device_id=peer, device_id_type=MESH)

    def local(i, src, dst):
        copy = pltpu.make_async_copy(src, dst, loc_s.at[i])
        copy.start()
        return copy

    loc_q = [local(c, q_hbm.at[c], q_all.at[0, c, 0]) for c in (0, 1)]
    loc_m = [local(2, list_hbm, list_ref), local(3, map_hbm, map_ref), local(4, pos_hbm, meta.at[pl.ds(0, 8)])]
    loc_w = [local(5, w_hbm, w_ref), local(6, prop_hbm, prop_ref)]

    for copy in loc_m:
        copy.wait()
    short = list_ref.shape[1]
    sub = lax.broadcasted_iota(I32, (short, short), 0)
    lane = lax.broadcasted_iota(I32, (short, short), 1)
    list_col = jnp.sum(jnp.where(sub == lane, list_ref[...], 0), axis=1, keepdims=True)
    sub = lax.broadcasted_iota(I32, (short, 128), 0)
    lane = lax.broadcasted_iota(I32, (short, 128), 1)
    stored = jnp.sum(jnp.where(list_col == lane, map_ref[...], 0), axis=1, keepdims=True)
    meta[pl.ds(8, 8), :] = jnp.broadcast_to(
        jnp.sum(jnp.where(stored == lane, sub + 1, 0), axis=0, keepdims=True) - 1, (8, 128)
    )
    meta_all[0, 0] = meta[...]

    pl.semaphore_wait(barrier, len(peers))

    def remote(src, dst, ss, rs, dev):
        return pltpu.make_async_remote_copy(
            src_ref=src, dst_ref=dst, send_sem=ss, recv_sem=rs, device_id=dev, device_id_type=MESH
        )

    started = []

    def go(copy):
        copy.start()
        started.append(copy)
        return copy

    lo, hi = pl.ds(0, QUART), pl.ds(QUART, QUART)
    ag = {}

    def ag_send(c, slot, kind, src, dst, dev):
        ag[c, slot, kind] = go(remote(src, dst, ag_ss.at[c, slot, kind], ag_rs.at[c, slot, kind], dev))

    def p1a(c):
        ag_send(c, 4, 0, q_all.at[0, c, 0], q_all.at[0, c, 3], slow(c, 1))
        ag_send(c, 4, 1, q_all.at[0, c, 0], q_all.at[0, c, 1], slow(c, -1))

    def p1b(c, kind):
        ag[c, 4, kind].wait_recv()
        if kind == 0:
            ag_send(c, 4, 2, q_all.at[0, c, 3, lo], q_all.at[0, c, 2, lo], slow(c, 1))
        else:
            ag_send(c, 4, 3, q_all.at[0, c, 1, hi], q_all.at[0, c, 2, hi], slow(c, -1))

    def p2a(c, j):
        ag_send(c, j, 0, q_all.at[0, c, j], q_all.at[3, c, j], fast(c, 1))
        ag_send(c, j, 1, q_all.at[0, c, j], q_all.at[1, c, j], fast(c, -1))

    def p2b(c, j):
        ag[c, j, 0].wait_recv()
        ag_send(c, j, 2, q_all.at[3, c, j, lo], q_all.at[2, c, j, lo], fast(c, 1))
        ag[c, j, 1].wait_recv()
        ag_send(c, j, 3, q_all.at[1, c, j, hi], q_all.at[2, c, j, hi], fast(c, -1))

    for copy in loc_q:
        copy.wait()
    p1a(0)
    p1a(1)
    meta_x = [
        go(remote(meta, meta_all.at[SIDE - a, 0], me_ss.at[0, a], me_rs.at[0, a], at(a, 0)))
        for a in (1, 2, 3)
    ]
    p2a(0, 0)
    p2a(1, 0)
    for copy in meta_x:
        copy.wait_recv()
    meta_y = [
        go(remote(meta_all.at[:, 0], meta_all.at[:, SIDE - a], me_ss.at[1, a], me_rs.at[1, a], at(0, a)))
        for a in (1, 2, 3)
    ]
    for copy in loc_w:
        copy.wait()
    inv[...] = grad_scale / prop_ref[...]
    words_t[...] = jnp.zeros_like(words_t)
    for c in (0, 1):
        p1b(c, 0)
        p1b(c, 1)
    for c in (0, 1):
        p2a(c, 3)
        p2a(c, 1)
    for copy in meta_y:
        copy.wait_recv()

    def prepare(d, carry):
        tile = meta_all[d // SIDE, d % SIDE]
        sub = lax.broadcasted_iota(I32, (QUART, 128), 0)
        lane = lax.broadcasted_iota(I32, (QUART, 128), 1)
        row = tile[8:9, :]
        entry = jnp.sum(jnp.where(lane == label * 8 + sub // 4, row, 0), axis=1, keepdims=True)
        base = jnp.where(entry >= 0, entry * 128 + (sub % 4) * 32, FAR)
        words = jnp.zeros((QUART, 128), I32)
        for p in range(8):
            rel = tile[p : p + 1, :] - base
            words = words | jnp.where((rel >= 0) & (rel < 32), jnp.left_shift(1, rel & 31), 0)
        words_t[d, :, 0:QUART] = jnp.transpose(words)
        sub8 = lax.broadcasted_iota(I32, (8, 128), 0)
        lane8 = lax.broadcasted_iota(I32, (8, 128), 1)
        entry8 = jnp.sum(jnp.where(lane8 == label * 8 + sub8, row, 0), axis=1, keepdims=True)
        live[d] = jnp.broadcast_to(jnp.where(entry8 >= 0, 0.5 * grad_scale, 0.0), (8, 128))
        return carry

    lax.fori_loop(0, SIDE * SIDE, prepare, 0)
    for c in (0, 1):
        ag[c, 4, 2].wait_recv()
        ag[c, 4, 3].wait_recv()
        p2a(c, 2)

    def tile_of(n):
        return pl.ds(pl.multiple_of(n * WIDE, WIDE), WIDE)

    def loop(body):
        def step(n, carry):
            body(n)
            return carry

        lax.fori_loop(0, TILES, step, 0)

    def score_chunk(k):
        def body(n):
            s = lax.dot_general(
                q_all[k].reshape(rows_all, dim), w_ref[tile_of(n), :],
                (((1,), (1,)), ((), ())), preferred_element_type=F32,
            )
            lane = lax.broadcasted_iota(I32, (HALF, 128), 1)
            up = 31 - (lane & 31)
            for c in (0, 1):
                for j in range(SIDE):
                    dev = j * SIDE + k if c == 0 else k * SIDE + j
                    r0 = (c * SIDE + j) * HALF
                    words = words_t[dev, c * HALF : (c + 1) * HALF, :]
                    for b in (0, 1):
                        cl = live[dev, pl.ds(2 * n + b, 1), :]
                        iv = inv[pl.ds(2 * n + b, 1), :]
                        pick = jnp.take_along_axis(words, (2 * n + b) * 4 + (lane >> 5), axis=1)
                        hit = jnp.left_shift(pick, up) < 0
                        t = jnp.tanh(0.5 * s[r0 : r0 + HALF, b * 128 : (b + 1) * 128])
                        g = t * cl + cl - jnp.where(hit, iv, 0.0)
                        sg[k, r0 : r0 + HALF, pl.ds(pl.multiple_of(n * WIDE + b * 128, 128), 128)] = g.astype(BF16)

        loop(body)

    def s1_copy(c, d, m, n):
        return remote(
            s1s.at[c, d, m, n], s1r.at[c, d, m, n], s1_ss.at[c, d, m, n], s1_rs.at[c, d, m, n], fast(c, 1 - 2 * d)
        )

    def query_chunk(k):
        def body(n):
            out = jnp.dot(sg[k], w_ref[:, tile_of(n)], preferred_element_type=F32)
            out = out.reshape(2, SIDE, HALF, WIDE)
            low, high = out[:, :, :QUART], out[:, :, QUART:]
            if k == 0:
                p0[n] = out
            for c in (0, 1):
                if k == 2:
                    s1s[c, 0, 0, n] = low[c].astype(BF16)
                    s1s[c, 1, 0, n] = high[c].astype(BF16)
                if k == 1:
                    p1[n, c] = low[c]
                    s1s[c, 0, 1, n] = high[c].astype(BF16)
                if k == 3:
                    p3[n, c] = high[c]
                    s1s[c, 1, 1, n] = low[c].astype(BF16)
            for c in (0, 1):
                if k in (1, 2):
                    s1_copy(c, 0, 2 - k, n).start()
                if k in (3, 2):
                    s1_copy(c, 1, 1 if k == 3 else 0, n).start()

        loop(body)

    def weight_tile(n, ks):
        out = None
        for k in ks:
            one = lax.dot_general(
                sg[k, :, tile_of(n)], q_all[k].reshape(rows_all, dim),
                (((0,), (0,)), ((), ())), preferred_element_type=F32,
            )
            out = one if out is None else out + one
        return out.reshape(2, RING, 2, 8, dim)

    def weight_first(n):
        wg[pl.ds(2 * n, 2)] = weight_tile(n, (0,))

    def x_copy(n):
        rows = pl.ds(2 * n, 2)
        return remote(wg.at[rows, :, 1 - core], xr.at[rows], x_ss.at[n], x_rs.at[n], other)

    def weight_last(n):
        rows = pl.ds(2 * n, 2)
        wg[rows] = wg[rows] + weight_tile(n, (3, 1, 2))
        x_copy(n).start()

    score_chunk(0)
    for c in (0, 1):
        p2b(c, 0)
    query_chunk(0)
    for c in (0, 1):
        p2b(c, 3)
        p2b(c, 1)
    loop(weight_first)
    for c in (0, 1):
        p2b(c, 2)
    score_chunk(3)
    query_chunk(3)
    score_chunk(1)
    query_chunk(1)
    for c in (0, 1):
        for j in range(SIDE):
            ag[c, j, 2].wait_recv()
            ag[c, j, 3].wait_recv()
    score_chunk(2)
    query_chunk(2)
    loop(weight_last)

    def z_copy(d, t, h):
        src, dst = (zs.at[d, t, h], zr.at[d, t, h]) if t < 3 else (zfs.at[d, h], zfr.at[d, h])
        return remote(src, dst, z_ss.at[d, t, h], z_rs.at[d, t, h], zdev(1 - 2 * d))

    def piece(r, h):
        i = lax.rem(z + r, RING)
        rows = slice(4 * h, 4 * h + 4)
        return (wg[rows, i, core] + xr[rows, i]).reshape(QUART, dim)

    def z_step(d, t, h):
        value = piece(4 - t if d == 0 else 4 + t, h)
        if t > (h if d == 0 else 1 - h):
            z_copy(d, t - 1, h).wait_recv()
            value = value + zr[d, t - 1, h].astype(F32)
        if t < 3:
            zs[d, t, h] = value.astype(BF16)
        else:
            zfs[d, h] = value
        go(z_copy(d, t, h))

    def s1_mid(n):
        for c in (0, 1):
            for d, keep in ((0, p1), (1, p3)):
                s1_copy(c, d, 0, n).wait_recv()
                s1s[c, d, 2, n] = (keep[n, c] + s1r[c, d, 0, n].astype(F32)).astype(BF16)
                go(s1_copy(c, d, 2, n))

    def s2_copy(c, d, n):
        return remote(s2s.at[c, d, n], s2r.at[c, d, n], s2_ss.at[c, d, 0, n], s2_rs.at[c, d, 0, n], slow(c, 1 - 2 * d))

    def s3_copy(c, d, n):
        return remote(s3s.at[c, d, n], s3r.at[c, d, n], s2_ss.at[c, d, 1, n], s2_rs.at[c, d, 1, n], slow(c, 1 - 2 * d))

    def s1_end(n):
        for c in (0, 1):
            for d in (0, 1):
                s1_copy(c, d, 1, n).wait_recv()
                s1_copy(c, d, 2, n).wait_recv()
            low = p0[n, c, :, :QUART] + s1r[c, 1, 1, n].astype(F32) + s1r[c, 0, 2, n].astype(F32)
            high = p0[n, c, :, QUART:] + s1r[c, 0, 1, n].astype(F32) + s1r[c, 1, 2, n].astype(F32)
            s2s[c, 0, n, 0] = low[2].astype(BF16)
            s2s[c, 0, n, 1] = high[1].astype(BF16)
            go(s2_copy(c, 0, n))
            s2s[c, 1, n, 0] = high[2].astype(BF16)
            s2s[c, 1, n, 1] = low[3].astype(BF16)
            go(s2_copy(c, 1, n))
            p0[n, c, 0, :QUART] = low[0]
            p0[n, c, 0, QUART:] = high[0]
            p1[n, c, 0] = low[1]
            p3[n, c, 0] = high[3]

    def s2_mid(n):
        for c in (0, 1):
            for d, keep in ((0, p1), (1, p3)):
                s2_copy(c, d, n).wait_recv()
                s3s[c, d, n] = keep[n, c, 0] + s2r[c, d, n, 0].astype(F32)
                go(s3_copy(c, d, n))

    def s2_end(n):
        cols = slice(n * WIDE, (n + 1) * WIDE)
        for c in (0, 1):
            s3_copy(c, 0, n).wait_recv()
            s3_copy(c, 1, n).wait_recv()
            qg_ref[c, :QUART, cols] = p0[n, c, 0, :QUART] + s2r[c, 1, n, 1].astype(F32) + s3r[c, 0, n]
            qg_ref[c, QUART:, cols] = p0[n, c, 0, QUART:] + s2r[c, 0, n, 1].astype(F32) + s3r[c, 1, n]

    for n in range(TILES):
        x_copy(n).wait_recv()
    z_step(0, 0, 0)
    z_step(1, 0, 1)
    z_step(0, 1, 1)
    z_step(1, 1, 0)
    s1_mid(0)
    s1_mid(1)
    z_step(0, 1, 0)
    z_step(1, 1, 1)
    s1_mid(2)
    s1_mid(3)
    z_step(0, 2, 1)
    z_step(1, 2, 0)
    s1_end(0)
    z_step(0, 2, 0)
    z_step(1, 2, 1)
    s1_end(1)
    z_step(0, 3, 1)
    z_step(1, 3, 0)
    s1_end(2)
    z_step(0, 3, 0)
    z_step(1, 3, 1)
    s1_end(3)
    for n in range(TILES):
        s2_mid(n)
    for n in range(TILES):
        s2_end(n)
    for h in (0, 1):
        z_copy(0, 3, h).wait_recv()
        z_copy(1, 3, h).wait_recv()
        wo_ref[4 * h : 4 * h + 4] = (piece(0, h) + zfr[0, h] + zfr[1, h]).reshape(4, 8, dim)
    for n in range(TILES):
        x_copy(n).wait_send()
        for c in (0, 1):
            for d in (0, 1):
                for m in (0, 1):
                    s1_copy(c, d, m, n).wait_send()
    for copy in started:
        copy.wait_send()


def per_device(queries, label_weights, propensity, positives, shortlist, owner_map):
    blocks, block_rows, dim = label_weights.shape
    hbm = pl.BlockSpec(memory_space=pl.ANY)
    vm = pl.BlockSpec(memory_space=pltpu.VMEM)
    dma = pltpu.SemaphoreType.DMA
    rows_all = 2 * SIDE * HALF
    qg, wo = pl.pallas_call(
        kernel,
        out_shape=(
            jax.ShapeDtypeStruct((2, HALF, dim), F32),
            jax.ShapeDtypeStruct((blocks, 8, dim), F32),
        ),
        in_specs=[hbm] * 6,
        out_specs=(vm, vm),
        scratch_shapes=[
            pltpu.VMEM((SIDE, 2, SIDE, HALF, dim), BF16),
            pltpu.VMEM((blocks * block_rows, dim), BF16),
            pltpu.VMEM((blocks, block_rows), F32),
            pltpu.VMEM((1, shortlist.shape[1]), I32),
            pltpu.VMEM((1, 128), I32),
            pltpu.VMEM((16, 128), I32),
            pltpu.VMEM((SIDE, SIDE, 16, 128), I32),
            pltpu.VMEM((SIDE * SIDE, 128, 128), I32),
            pltpu.VMEM((SIDE * SIDE, 8, 128), F32),
            pltpu.VMEM((8, 128), F32),
            pltpu.VMEM((SIDE, rows_all, blocks * block_rows), BF16),
            pltpu.VMEM((TILES, 2, SIDE, HALF, WIDE), F32),
            pltpu.VMEM((TILES, 2, SIDE, QUART, WIDE), F32),
            pltpu.VMEM((TILES, 2, SIDE, QUART, WIDE), F32),
            pltpu.VMEM((blocks, RING, 2, 8, dim), F32),
            pltpu.VMEM((2, 2, 3, TILES, SIDE, QUART, WIDE), BF16),
            pltpu.VMEM((2, 2, 3, TILES, SIDE, QUART, WIDE), BF16),
            pltpu.VMEM((2, 2, TILES, 2, QUART, WIDE), BF16),
            pltpu.VMEM((2, 2, TILES, 2, QUART, WIDE), BF16),
            pltpu.VMEM((2, 2, TILES, QUART, WIDE), F32),
            pltpu.VMEM((2, 2, TILES, QUART, WIDE), F32),
            pltpu.VMEM((blocks, RING, 8, dim), F32),
            pltpu.VMEM((2, 3, 2, QUART, dim), BF16),
            pltpu.VMEM((2, 3, 2, QUART, dim), BF16),
            pltpu.VMEM((2, 2, QUART, dim), F32),
            pltpu.VMEM((2, 2, QUART, dim), F32),
            dma((7,)),
            dma((2, 4)), dma((2, 4)),
            dma((2, 5, 4)), dma((2, 5, 4)),
            dma((2, 2, 3, TILES)), dma((2, 2, 3, TILES)),
            dma((2, 2, 2, TILES)), dma((2, 2, 2, TILES)),
            dma((TILES,)), dma((TILES,)),
            dma((2, 4, 2)), dma((2, 4, 2)),
        ],
        compiler_params=pltpu.CompilerParams(
            collective_id=0, has_side_effects=True, vmem_limit_bytes=60 * 1024 * 1024
        ),
    )(
        queries.reshape(2, HALF, dim),
        label_weights.reshape(blocks * block_rows, dim),
        propensity,
        positives.T,
        shortlist,
        owner_map.reshape(1, -1),
    )
    return qg.reshape(2 * HALF, dim), wo


def solution(mesh):
    in_specs = (
        P(("dp", "label", "section"), None),
        P("label", None, None),
        P("label", None),
        P(("dp", "label", "section"), None),
        P(("dp", "label"), None),
        P(),
    )
    out_specs = (P(("dp", "label", "section"), None), P("label", ("dp", "section"), None))
    return jax.shard_map(
        per_device, mesh=mesh, in_specs=in_specs, out_specs=out_specs, check_vma=False
    )
```

```python
import jax
import jax.numpy as jnp
from jax import lax
from jax.experimental import pallas as pl
from jax.experimental.pallas import tpu as pltpu
from jax.sharding import PartitionSpec as P

MESH = pl.DeviceIdType.MESH
SIDE = 4
RING = 8
HALF = 64
QUART = 32
TILES = 4
WIDE = 256
FAR = 1 << 20
grad_scale = 0.25
F32, BF16, I32 = jnp.float32, jnp.bfloat16, jnp.int32


def kernel(
    q_hbm, w_hbm, prop_hbm, pos_hbm, list_hbm, map_hbm, qg_ref, wo_ref,
    q_all, w_ref, prop_ref, list_ref, map_ref, meta, meta_all, words_t, live, inv,
    sg, p0, p1, p3, wg, s1s, s1r, s2s, s2r, s3s, s3r, xr, zs, zr, zfs, zfr,
    loc_s, me_ss, me_rs, ag_ss, ag_rs, s1_ss, s1_rs, s2_ss, s2_rs, x_ss, x_rs, z_ss, z_rs,
):
    label = lax.axis_index("label")
    z = lax.axis_index("dp")
    core = lax.axis_index("section")
    x, y = label // SIDE, label % SIDE
    dim = SIDE * WIDE

    def at(dx, dy):
        return {"label": lax.rem(x + dx + SIDE, SIDE) * SIDE + lax.rem(y + dy + SIDE, SIDE)}

    def along(axis, d):
        return at(d, 0) if axis == 0 else at(0, d)

    def slow(c, d):
        return along(c, d)

    def fast(c, d):
        return along(1 - c, d)

    def zdev(d):
        return {"dp": lax.rem(z + d + RING, RING)}

    other = {"section": 1 - core}

    peers = [at(d, 0) for d in (1, 2, 3)] + [at(0, d) for d in (1, 2, 3)] + [zdev(1), zdev(-1), other]
    barrier = pltpu.get_barrier_semaphore()
    for peer in peers:
        pl.semaphore_signal(barrier, inc=1, device_id=peer, device_id_type=MESH)

    def local(i, src, dst):
        copy = pltpu.make_async_copy(src, dst, loc_s.at[i])
        copy.start()
        return copy

    loc_q = [local(c, q_hbm.at[c], q_all.at[c]) for c in (0, 1)]
    loc_m = [local(2, list_hbm, list_ref), local(3, map_hbm, map_ref), local(4, pos_hbm, meta.at[pl.ds(0, 8)])]
    loc_w = [local(5, w_hbm, w_ref), local(6, prop_hbm, prop_ref)]

    pl.semaphore_wait(barrier, len(peers))

    def remote(src, dst, ss, rs, dev):
        return pltpu.make_async_remote_copy(
            src_ref=src, dst_ref=dst, send_sem=ss, recv_sem=rs, device_id=dev, device_id_type=MESH
        )

    started = []

    def go(copy):
        copy.start()
        started.append(copy)
        return copy

    def blocks_of(ks, js):
        return [(k, c, j) for k in ks for j in js for c in (0, 1)]

    chunk_a = blocks_of((0,), (0, 3, 1))
    chunk_b = blocks_of((0,), (2,)) + blocks_of((3, 1), (0,))
    chunk_c = blocks_of((3, 1), (3, 1))
    chunk_d = blocks_of((3, 1), (2,))
    chunk_e = blocks_of((2,), (0, 3))
    chunk_f = blocks_of((2,), (1, 2))
    order = chunk_a + chunk_b + chunk_c + chunk_d + chunk_e + chunk_f

    def slot_of(k, c, j):
        return order.index((k, c, j))

    def qa(k, c, j, rows=None):
        ref = q_all.at[slot_of(k, c, j)]
        return ref if rows is None else ref.at[rows]

    lo, hi = pl.ds(0, QUART), pl.ds(QUART, QUART)
    ag = {}

    def ag_send(c, slot, kind, src, dst, dev):
        ag[c, slot, kind] = go(remote(src, dst, ag_ss.at[c, slot, kind], ag_rs.at[c, slot, kind], dev))

    def p1a(c):
        ag_send(c, 4, 0, qa(0, c, 0), qa(0, c, 3), slow(c, 1))
        ag_send(c, 4, 1, qa(0, c, 0), qa(0, c, 1), slow(c, -1))

    def p1b(c, kind):
        ag[c, 4, kind].wait_recv()
        if kind == 0:
            ag_send(c, 4, 2, qa(0, c, 3, lo), qa(0, c, 2, lo), slow(c, 1))
        else:
            ag_send(c, 4, 3, qa(0, c, 1, hi), qa(0, c, 2, hi), slow(c, -1))

    def p2a(c, j):
        ag_send(c, j, 0, qa(0, c, j), qa(3, c, j), fast(c, 1))
        ag_send(c, j, 1, qa(0, c, j), qa(1, c, j), fast(c, -1))

    def p2b(c, j):
        ag[c, j, 0].wait_recv()
        ag_send(c, j, 2, qa(3, c, j, lo), qa(2, c, j, lo), fast(c, 1))
        ag[c, j, 1].wait_recv()
        ag_send(c, j, 3, qa(1, c, j, hi), qa(2, c, j, hi), fast(c, -1))

    for copy in loc_q:
        copy.wait()
    p1a(0)
    p1a(1)

    for copy in loc_m:
        copy.wait()
    short = list_ref.shape[1]
    sub = lax.broadcasted_iota(I32, (short, short), 0)
    lane = lax.broadcasted_iota(I32, (short, short), 1)
    list_col = jnp.sum(jnp.where(sub == lane, list_ref[...], 0), axis=1, keepdims=True)
    sub = lax.broadcasted_iota(I32, (short, 128), 0)
    lane = lax.broadcasted_iota(I32, (short, 128), 1)
    stored = jnp.sum(jnp.where(list_col == lane, map_ref[...], 0), axis=1, keepdims=True)
    meta[pl.ds(8, 8), :] = jnp.broadcast_to(
        jnp.sum(jnp.where(stored == lane, sub + 1, 0), axis=0, keepdims=True) - 1, (8, 128)
    )
    meta_all[0, 0] = meta[...]

    meta_x = [go(remote(meta, meta_all.at[SIDE - a, 0], me_ss.at[0, a], me_rs.at[0, a], at(a, 0))) for a in (1, 3, 2)]
    meta_y = [go(remote(meta, meta_all.at[0, SIDE - a], me_ss.at[1, a], me_rs.at[1, a], at(0, a))) for a in (1, 3, 2)]
    p2a(0, 0)
    p2a(1, 0)
    words_t[...] = jnp.zeros_like(words_t)
    for copy in loc_w:
        copy.wait()
    inv[...] = grad_scale / prop_ref[...]
    for c in (0, 1):
        p1b(c, 0)
        p1b(c, 1)
    for copy in meta_x:
        copy.wait_recv()
    far = pl.ds(1, SIDE - 1)
    meta_xy = [
        go(remote(meta_all.at[far, 0], meta_all.at[far, SIDE - a], me_ss.at[2, a], me_rs.at[2, a], at(0, a)))
        for a in (1, 3, 2)
    ]
    for c in (0, 1):
        p2a(c, 3)
        p2a(c, 1)
    for copy in meta_y:
        copy.wait_recv()

    def prepare(d):
        tile = meta_all[d // SIDE, d % SIDE]
        sub = lax.broadcasted_iota(I32, (QUART, 128), 0)
        lane = lax.broadcasted_iota(I32, (QUART, 128), 1)
        row = tile[8:9, :]
        entry = jnp.sum(jnp.where(lane == label * 8 + sub // 4, row, 0), axis=1, keepdims=True)
        base = jnp.where(entry >= 0, entry * 128 + (sub % 4) * 32, FAR)
        words = jnp.zeros((QUART, 128), I32)
        for p in range(8):
            rel = tile[p : p + 1, :] - base
            words = words | jnp.where((rel >= 0) & (rel < 32), jnp.left_shift(1, rel & 31), 0)
        words_t[d, :, 0:QUART] = jnp.transpose(words)
        sub8 = lax.broadcasted_iota(I32, (8, 128), 0)
        lane8 = lax.broadcasted_iota(I32, (8, 128), 1)
        entry8 = jnp.sum(jnp.where(lane8 == label * 8 + sub8, row, 0), axis=1, keepdims=True)
        live[d] = jnp.broadcast_to(jnp.where(entry8 >= 0, 0.5 * grad_scale, 0.0), (8, 128))

    for d in range(SIDE * SIDE):
        if d < SIDE or d % SIDE == 0:
            prepare(d)

    def tile_of(n):
        return pl.ds(n * WIDE, WIDE)

    def loop(body):
        for n in range(TILES):
            body(n)

    def rows_of(group):
        return pl.ds(slot_of(*group[0]) * HALF, len(group) * HALF)

    def queries_of(group):
        first = slot_of(*group[0])
        return q_all[first : first + len(group)].reshape(len(group) * HALF, dim)

    def score_chunk(group):
        first = slot_of(*group[0])

        def body(n):
            s = lax.dot_general(
                queries_of(group), w_ref[tile_of(n), :], (((1,), (1,)), ((), ())), preferred_element_type=F32
            )
            lane = lax.broadcasted_iota(I32, (HALF, 128), 1)
            up = 31 - (lane & 31)
            for i, (k, c, j) in enumerate(group):
                dev = j * SIDE + k if c == 0 else k * SIDE + j
                r0 = i * HALF
                words = words_t[dev, c * HALF : (c + 1) * HALF, :]
                for b in (0, 1):
                    cl = live[dev, pl.ds(2 * n + b, 1), :]
                    iv = inv[pl.ds(2 * n + b, 1), :]
                    pick = jnp.take_along_axis(words, (2 * n + b) * 4 + (lane >> 5), axis=1)
                    hit = jnp.left_shift(pick, up) < 0
                    t = jnp.tanh(0.5 * s[r0 : r0 + HALF, b * 128 : (b + 1) * 128])
                    g = t * cl + cl - jnp.where(hit, iv, 0.0)
                    cols = pl.ds(n * WIDE + b * 128, 128)
                    sg[pl.ds((first + i) * HALF, HALF), cols] = g.astype(BF16)

        loop(body)

    def s1_copy(c, d, m, n):
        return remote(
            s1s.at[c, d, m, n], s1r.at[c, d, m, n], s1_ss.at[c, d, m, n], s1_rs.at[c, d, m, n], fast(c, 1 - 2 * d)
        )

    def query_chunk(group, send):
        def body(n):
            out = jnp.dot(sg[rows_of(group), :], w_ref[:, tile_of(n)], preferred_element_type=F32)
            for i, (k, c, j) in enumerate(group):
                low, high = out[i * HALF : i * HALF + QUART], out[i * HALF + QUART : (i + 1) * HALF]
                if k == 0:
                    p0[n, c, j] = out[i * HALF : (i + 1) * HALF]
                if k == 2:
                    s1s[c, 0, 0, n, j] = low.astype(BF16)
                    s1s[c, 1, 0, n, j] = high.astype(BF16)
                if k == 1:
                    p1[n, c, j] = low
                    s1s[c, 0, 1, n, j] = high.astype(BF16)
                if k == 3:
                    p3[n, c, j] = high
                    s1s[c, 1, 1, n, j] = low.astype(BF16)
            if send is not None:
                for c in (0, 1):
                    for d in (0, 1):
                        s1_copy(c, d, send, n).start()

        loop(body)

    def weight_tile(n, group):
        return lax.dot_general(
            sg[rows_of(group), tile_of(n)], queries_of(group),
            (((0,), (0,)), ((), ())), preferred_element_type=F32,
        ).reshape(2, RING, 2, 8, dim)

    def x_copy(n):
        rows = pl.ds(2 * n, 2)
        return remote(wg.at[rows, :, 1 - core], xr.at[rows], x_ss.at[n], x_rs.at[n], other)

    def weight_chunk(group):
        def body(n):
            rows = pl.ds(2 * n, 2)
            if group[0] == chunk_a[0]:
                wg[rows] = weight_tile(n, group)
            else:
                wg[rows] = wg[rows] + weight_tile(n, group)
            if group[-1] == chunk_f[-1]:
                x_copy(n).start()

        loop(body)

    score_chunk(chunk_a)
    query_chunk(chunk_a, None)
    for copy in meta_xy:
        copy.wait_recv()
    for d in range(SIDE * SIDE):
        if d >= SIDE and d % SIDE:
            prepare(d)
    for c in (0, 1):
        ag[c, 4, 2].wait_recv()
        ag[c, 4, 3].wait_recv()
        p2a(c, 2)
    for c in (0, 1):
        p2b(c, 0)
    score_chunk(chunk_b)
    query_chunk(chunk_b, None)
    for c in (0, 1):
        p2b(c, 3)
    weight_chunk(chunk_a + chunk_b)
    for c in (0, 1):
        p2b(c, 1)
    score_chunk(chunk_c)
    query_chunk(chunk_c, None)
    for c in (0, 1):
        p2b(c, 2)
    score_chunk(chunk_d)
    query_chunk(chunk_d, 1)
    weight_chunk(chunk_c + chunk_d)
    for j in (0, 3):
        for c in (0, 1):
            ag[c, j, 2].wait_recv()
            ag[c, j, 3].wait_recv()
    score_chunk(chunk_e)
    query_chunk(chunk_e, None)
    for j in (1, 2):
        for c in (0, 1):
            ag[c, j, 2].wait_recv()
            ag[c, j, 3].wait_recv()
    score_chunk(chunk_f)
    query_chunk(chunk_f, 0)
    weight_chunk(chunk_e + chunk_f)

    def z_copy(d, t, n):
        sem = (z_ss.at[d, t, n], z_rs.at[d, t, n], zdev(1 - 2 * d))
        if t == 0:
            return remote(zs.at[d, 2, n, pl.ds(0, 8)], zr.at[d, 2, n, pl.ds(0, 8)], *sem)
        if t < 3:
            return remote(zs.at[d, t - 1, n], zr.at[d, t - 1, n], *sem)
        return remote(zfs.at[d, n], zfr.at[d, n], *sem)

    def piece(r, n):
        i = lax.rem(z + r, RING)
        rows = slice(2 * n, 2 * n + 2)
        return wg[rows, i, core] + xr[rows, i]

    def z_step(d, t, n):
        if t == 0:
            i = lax.rem(z + 4, RING)
            zs[d, 2, n, 0:8] = (wg[2 * n + d, i, core] + xr[2 * n + d, i]).astype(BF16)
        else:
            value = piece(4 - t if d == 0 else 4 + t, n)
            z_copy(d, t - 1, n).wait_recv()
            if t == 1:
                came = zr[d, 2, n, 0:8].astype(F32)
                none = jnp.zeros_like(came)
                value = value + jnp.stack([came, none] if d == 0 else [none, came])
            else:
                value = value + zr[d, t - 2, n].astype(F32).reshape(2, 8, dim)
            value = value.reshape(16, dim)
            if t < 3:
                zs[d, t - 1, n] = value.astype(BF16)
            else:
                zfs[d, n] = value
        go(z_copy(d, t, n))

    def z_hop(t, n):
        z_step(0, t, n)
        z_step(1, t, n)

    def s1_mid(n):
        for c in (0, 1):
            for d, keep in ((0, p1), (1, p3)):
                s1_copy(c, d, 0, n).wait_recv()
                s1s[c, d, 2, n] = (keep[n, c] + s1r[c, d, 0, n].astype(F32)).astype(BF16)
                go(s1_copy(c, d, 2, n))

    def s2_copy(c, d, n):
        return remote(s2s.at[c, d, n], s2r.at[c, d, n], s2_ss.at[c, d, 0, n], s2_rs.at[c, d, 0, n], slow(c, 1 - 2 * d))

    def s3_copy(c, d, n):
        return remote(s3s.at[c, d, n], s3r.at[c, d, n], s2_ss.at[c, d, 1, n], s2_rs.at[c, d, 1, n], slow(c, 1 - 2 * d))

    def s1_end(n):
        for c in (0, 1):
            for d in (0, 1):
                s1_copy(c, d, 1, n).wait_recv()
                s1_copy(c, d, 2, n).wait_recv()
            low = p0[n, c, :, :QUART] + s1r[c, 1, 1, n].astype(F32) + s1r[c, 0, 2, n].astype(F32)
            high = p0[n, c, :, QUART:] + s1r[c, 0, 1, n].astype(F32) + s1r[c, 1, 2, n].astype(F32)
            s2s[c, 0, n, 0] = low[2].astype(BF16)
            s2s[c, 0, n, 1] = high[1].astype(BF16)
            go(s2_copy(c, 0, n))
            s2s[c, 1, n, 0] = high[2].astype(BF16)
            s2s[c, 1, n, 1] = low[3].astype(BF16)
            go(s2_copy(c, 1, n))
            p0[n, c, 0, :QUART] = low[0]
            p0[n, c, 0, QUART:] = high[0]
            p1[n, c, 0] = low[1]
            p3[n, c, 0] = high[3]

    def s2_mid(n):
        for c in (0, 1):
            for d, keep in ((0, p1), (1, p3)):
                s2_copy(c, d, n).wait_recv()
                s3s[c, d, n] = keep[n, c, 0] + s2r[c, d, n, 0].astype(F32)
                go(s3_copy(c, d, n))

    def s2_end(n):
        cols = slice(n * WIDE, (n + 1) * WIDE)
        for c in (0, 1):
            s3_copy(c, 0, n).wait_recv()
            s3_copy(c, 1, n).wait_recv()
            qg_ref[c, :QUART, cols] = p0[n, c, 0, :QUART] + s2r[c, 1, n, 1].astype(F32) + s3r[c, 0, n]
            qg_ref[c, QUART:, cols] = p0[n, c, 0, QUART:] + s2r[c, 0, n, 1].astype(F32) + s3r[c, 1, n]

    for n in range(TILES):
        x_copy(n).wait_recv()
        z_hop(0, n)
    s1_mid(0)
    s1_mid(1)
    for n in range(TILES):
        z_hop(1, n)
    s1_mid(2)
    s1_mid(3)
    z_hop(2, 0)
    z_hop(2, 1)
    s1_end(0)
    z_hop(2, 2)
    z_hop(2, 3)
    s1_end(1)
    z_hop(3, 0)
    z_hop(3, 1)
    s1_end(2)
    z_hop(3, 2)
    z_hop(3, 3)
    s1_end(3)
    for n in range(TILES):
        s2_mid(n)
    for n in range(TILES):
        s2_end(n)
    for n in range(TILES):
        z_copy(0, 3, n).wait_recv()
        z_copy(1, 3, n).wait_recv()
        wo_ref[2 * n : 2 * n + 2] = piece(0, n) + (zfr[0, n] + zfr[1, n]).reshape(2, 8, dim)
    for n in range(TILES):
        x_copy(n).wait_send()
        for c in (0, 1):
            for d in (0, 1):
                for m in (0, 1):
                    s1_copy(c, d, m, n).wait_send()
    for copy in started:
        copy.wait_send()


def per_device(queries, label_weights, propensity, positives, shortlist, owner_map):
    blocks, block_rows, dim = label_weights.shape
    hbm = pl.BlockSpec(memory_space=pl.ANY)
    vm = pl.BlockSpec(memory_space=pltpu.VMEM)
    dma = pltpu.SemaphoreType.DMA
    qg, wo = pl.pallas_call(
        kernel,
        out_shape=(
            pltpu.VMEM((2, HALF, dim), F32),
            pltpu.VMEM((blocks, 8, dim), F32),
        ),
        in_specs=[hbm] * 6,
        out_specs=(vm, vm),
        scratch_shapes=[
            pltpu.VMEM((SIDE * 2 * SIDE, HALF, dim), BF16),
            pltpu.VMEM((blocks * block_rows, dim), BF16),
            pltpu.VMEM((blocks, block_rows), F32),
            pltpu.VMEM((1, shortlist.shape[1]), I32),
            pltpu.VMEM((1, 128), I32),
            pltpu.VMEM((16, 128), I32),
            pltpu.VMEM((SIDE, SIDE, 16, 128), I32),
            pltpu.VMEM((SIDE * SIDE, 128, 128), I32),
            pltpu.VMEM((SIDE * SIDE, 8, 128), F32),
            pltpu.VMEM((8, 128), F32),
            pltpu.VMEM((SIDE * 2 * SIDE * HALF, blocks * block_rows), BF16),
            pltpu.VMEM((TILES, 2, SIDE, HALF, WIDE), F32),
            pltpu.VMEM((TILES, 2, SIDE, QUART, WIDE), F32),
            pltpu.VMEM((TILES, 2, SIDE, QUART, WIDE), F32),
            pltpu.VMEM((blocks, RING, 2, 8, dim), F32),
            pltpu.VMEM((2, 2, 3, TILES, SIDE, QUART, WIDE), BF16),
            pltpu.VMEM((2, 2, 3, TILES, SIDE, QUART, WIDE), BF16),
            pltpu.VMEM((2, 2, TILES, 2, QUART, WIDE), BF16),
            pltpu.VMEM((2, 2, TILES, 2, QUART, WIDE), BF16),
            pltpu.VMEM((2, 2, TILES, QUART, WIDE), F32),
            pltpu.VMEM((2, 2, TILES, QUART, WIDE), F32),
            pltpu.VMEM((blocks, RING, 8, dim), F32),
            pltpu.VMEM((2, 3, TILES, 16, dim), BF16),
            pltpu.VMEM((2, 3, TILES, 16, dim), BF16),
            pltpu.VMEM((2, TILES, 16, dim), F32),
            pltpu.VMEM((2, TILES, 16, dim), F32),
            dma((7,)),
            dma((3, 4)), dma((3, 4)),
            dma((2, 5, 4)), dma((2, 5, 4)),
            dma((2, 2, 3, TILES)), dma((2, 2, 3, TILES)),
            dma((2, 2, 2, TILES)), dma((2, 2, 2, TILES)),
            dma((TILES,)), dma((TILES,)),
            dma((2, 4, TILES)), dma((2, 4, TILES)),
        ],
        compiler_params=pltpu.CompilerParams(
            collective_id=0, has_side_effects=True, vmem_limit_bytes=66_256_896
        ),
    )(
        queries.reshape(2, HALF, dim),
        label_weights.reshape(blocks * block_rows, dim),
        propensity,
        positives.T,
        shortlist,
        owner_map.reshape(1, -1),
    )
    return qg.reshape(2 * HALF, dim), wo


def solution(mesh):
    in_specs = (
        P(("dp", "label", "section"), None),
        P("label", None, None),
        P("label", None),
        P(("dp", "label", "section"), None),
        P(("dp", "label"), None),
        P(),
    )
    out_specs = (P(("dp", "label", "section"), None), P("label", ("dp", "section"), None))
    return jax.shard_map(
        per_device, mesh=mesh, in_specs=in_specs, out_specs=out_specs, check_vma=False
    )
```

```python
import jax
import jax.numpy as jnp
from jax import lax
from jax.experimental import pallas as pl
from jax.experimental.pallas import tpu as pltpu
from jax.sharding import PartitionSpec as P

MESH = pl.DeviceIdType.MESH
SIDE = 4
RING = 8
HALF = 64
QUART = 32
TILES = 4
WIDE = 256
FAR = 1 << 20
grad_scale = 0.25
F32, BF16, I32 = jnp.float32, jnp.bfloat16, jnp.int32


def kernel(
    q_hbm, w_hbm, prop_hbm, pos_hbm, list_hbm, map_hbm, qg_ref, wo_ref,
    q_all, w_ref, prop_ref, list_ref, map_ref, meta, meta_all, words_t, live, inv,
    sg, p0, p1, p3, wg, s1s, s1r, s2s, s2r, s3s, s3r, xr, zs, zr, zfs, zfr,
    loc_s, me_ss, me_rs, ag_ss, ag_rs, s1_ss, s1_rs, s2_ss, s2_rs, x_ss, x_rs, z_ss, z_rs, met,
):
    label = lax.axis_index("label")
    z = lax.axis_index("dp")
    core = lax.axis_index("section")
    x, y = label // SIDE, label % SIDE
    dim = SIDE * WIDE

    def at(dx, dy):
        return {"label": lax.rem(x + dx + SIDE, SIDE) * SIDE + lax.rem(y + dy + SIDE, SIDE)}

    def along(axis, d):
        return at(d, 0) if axis == 0 else at(0, d)

    def slow(c, d):
        return along(c, d)

    def fast(c, d):
        return along(1 - c, d)

    def zdev(d):
        return {"dp": lax.rem(z + d + RING, RING)}

    other = {"section": 1 - core}

    peers = [at(d, 0) for d in (1, 2, 3)] + [at(0, d) for d in (1, 2, 3)] + [other]
    odd = lax.rem(z, 2)
    barrier = pltpu.get_barrier_semaphore()
    for peer in peers:
        pl.semaphore_signal(barrier, inc=1, device_id=peer, device_id_type=MESH)

    @pl.when(odd == 0)
    def _():
        for d in (1, -1):
            pl.semaphore_signal(barrier, inc=1, device_id=zdev(d), device_id_type=MESH)


    def local(i, src, dst):
        copy = pltpu.make_async_copy(src, dst, loc_s.at[i])
        copy.start()
        return copy

    loc_q = [local(c, q_hbm.at[c], q_all.at[c]) for c in (0, 1)]
    loc_m = [local(2, list_hbm, list_ref), local(3, map_hbm, map_ref), local(4, pos_hbm, meta.at[pl.ds(0, 8)])]
    loc_w = [local(5, w_hbm, w_ref), local(6, prop_hbm, prop_ref)]

    for copy in loc_m:
        copy.wait()
    short = list_ref.shape[1]
    sub = lax.broadcasted_iota(I32, (short, short), 0)
    lane = lax.broadcasted_iota(I32, (short, short), 1)
    list_col = jnp.sum(jnp.where(sub == lane, list_ref[...], 0), axis=1, keepdims=True)
    sub = lax.broadcasted_iota(I32, (short, 128), 0)
    lane = lax.broadcasted_iota(I32, (short, 128), 1)
    stored = jnp.sum(jnp.where(list_col == lane, map_ref[...], 0), axis=1, keepdims=True)
    meta[pl.ds(8, 8), :] = jnp.broadcast_to(
        jnp.sum(jnp.where(stored == lane, sub + 1, 0), axis=0, keepdims=True) - 1, (8, 128)
    )
    meta_all[0, 0] = meta[...]

    pl.semaphore_wait(barrier, len(peers) + 2 * odd)

    @pl.when(odd == 1)
    def _():
        for d in (1, -1):
            pl.semaphore_signal(met, inc=1, device_id=zdev(d), device_id_type=MESH)


    def remote(src, dst, ss, rs, dev):
        return pltpu.make_async_remote_copy(
            src_ref=src, dst_ref=dst, send_sem=ss, recv_sem=rs, device_id=dev, device_id_type=MESH
        )

    started = []

    def go(copy):
        copy.start()
        started.append(copy)
        return copy

    def blocks_of(ks, js):
        return [(k, c, j) for k in ks for j in js for c in (0, 1)]

    chunk_a = blocks_of((0,), (0, 3, 1))
    chunk_b = blocks_of((0,), (2,)) + blocks_of((3, 1), (0,))
    chunk_c = blocks_of((3, 1), (3, 1))
    chunk_d = blocks_of((3, 1), (2,))
    chunk_e = blocks_of((2,), (0, 3))
    chunk_f = blocks_of((2,), (1, 2))
    order = chunk_a + chunk_b + chunk_c + chunk_d + chunk_e + chunk_f

    def slot_of(k, c, j):
        return order.index((k, c, j))

    def qa(k, c, j, rows=None):
        ref = q_all.at[slot_of(k, c, j)]
        return ref if rows is None else ref.at[rows]

    lo, hi = pl.ds(0, QUART), pl.ds(QUART, QUART)
    ag = {}

    def ag_send(c, slot, kind, src, dst, dev):
        ag[c, slot, kind] = go(remote(src, dst, ag_ss.at[c, slot, kind], ag_rs.at[c, slot, kind], dev))

    def p1a(c, slot):
        up, down = (lo, hi) if slot == 4 else (hi, lo)
        ag_send(c, slot, 0, qa(0, c, 0, up), qa(0, c, 3, up), slow(c, 1))
        ag_send(c, slot, 1, qa(0, c, 0, down), qa(0, c, 1, down), slow(c, -1))

    def p1b(c, kind):
        ag[c, 4, kind].wait_recv()
        if kind == 0:
            ag_send(c, 4, 2, qa(0, c, 3, lo), qa(0, c, 2, lo), slow(c, 1))
        else:
            ag_send(c, 4, 3, qa(0, c, 1, hi), qa(0, c, 2, hi), slow(c, -1))

    def p2a(c, j):
        ag_send(c, j, 0, qa(0, c, j), qa(3, c, j), fast(c, 1))
        ag_send(c, j, 1, qa(0, c, j), qa(1, c, j), fast(c, -1))

    def p2b(c, j):
        ag[c, j, 0].wait_recv()
        ag_send(c, j, 2, qa(3, c, j, lo), qa(2, c, j, lo), fast(c, 1))
        ag[c, j, 1].wait_recv()
        ag_send(c, j, 3, qa(1, c, j, hi), qa(2, c, j, hi), fast(c, -1))

    meta_x = [go(remote(meta, meta_all.at[SIDE - a, 0], me_ss.at[0, a], me_rs.at[0, a], at(a, 0))) for a in (1, 3, 2)]
    meta_y = [go(remote(meta, meta_all.at[0, SIDE - a], me_ss.at[1, a], me_rs.at[1, a], at(0, a))) for a in (1, 3, 2)]
    for copy in loc_q:
        copy.wait()
    p1a(0, 4)
    p1a(1, 4)
    p1a(0, 5)
    p1a(1, 5)
    words_t[...] = jnp.zeros_like(words_t)
    for copy in loc_w:
        copy.wait()
    inv[...] = grad_scale / prop_ref[...]
    for copy in meta_x:
        copy.wait_recv()
    far = pl.ds(1, SIDE - 1)
    meta_xy = [
        go(remote(meta_all.at[far, 0], meta_all.at[far, SIDE - a], me_ss.at[2, a], me_rs.at[2, a], at(0, a)))
        for a in (1, 3, 2)
    ]
    for c in (0, 1):
        p1b(c, 0)
        p1b(c, 1)
    p2a(0, 0)
    p2a(1, 0)
    for copy in meta_y:
        copy.wait_recv()

    def prepare(d):
        tile = meta_all[d // SIDE, d % SIDE]
        sub = lax.broadcasted_iota(I32, (QUART, 128), 0)
        lane = lax.broadcasted_iota(I32, (QUART, 128), 1)
        row = tile[8:9, :]
        entry = jnp.sum(jnp.where(lane == label * 8 + sub // 4, row, 0), axis=1, keepdims=True)
        base = jnp.where(entry >= 0, entry * 128 + (sub % 4) * 32, FAR)
        words = jnp.zeros((QUART, 128), I32)
        for p in range(8):
            rel = tile[p : p + 1, :] - base
            words = words | jnp.where((rel >= 0) & (rel < 32), jnp.left_shift(1, rel & 31), 0)
        words_t[d, :, 0:QUART] = jnp.transpose(words)
        sub8 = lax.broadcasted_iota(I32, (8, 128), 0)
        lane8 = lax.broadcasted_iota(I32, (8, 128), 1)
        entry8 = jnp.sum(jnp.where(lane8 == label * 8 + sub8, row, 0), axis=1, keepdims=True)
        live[d] = jnp.broadcast_to(jnp.where(entry8 >= 0, 0.5 * grad_scale, 0.0), (8, 128))

    for d in range(SIDE * SIDE):
        if d < SIDE or d % SIDE == 0:
            prepare(d)
    for c in (0, 1):
        ag[c, 5, 0].wait_recv()
        ag[c, 5, 1].wait_recv()
        p2a(c, 3)
        p2a(c, 1)

    def tile_of(n):
        return pl.ds(n * WIDE, WIDE)

    def loop(body):
        for n in range(TILES):
            body(n)

    def rows_of(group):
        return pl.ds(slot_of(*group[0]) * HALF, len(group) * HALF)

    def queries_of(group):
        first = slot_of(*group[0])
        return q_all[first : first + len(group)].reshape(len(group) * HALF, dim)

    def score_chunk(group):
        first = slot_of(*group[0])

        def body(n):
            s = lax.dot_general(
                queries_of(group), w_ref[tile_of(n), :], (((1,), (1,)), ((), ())), preferred_element_type=F32
            )
            lane = lax.broadcasted_iota(I32, (HALF, 128), 1)
            up = 31 - (lane & 31)
            for i, (k, c, j) in enumerate(group):
                dev = j * SIDE + k if c == 0 else k * SIDE + j
                r0 = i * HALF
                words = words_t[dev, c * HALF : (c + 1) * HALF, :]
                for b in (0, 1):
                    cl = live[dev, pl.ds(2 * n + b, 1), :]
                    iv = inv[pl.ds(2 * n + b, 1), :]
                    pick = jnp.take_along_axis(words, (2 * n + b) * 4 + (lane >> 5), axis=1)
                    hit = jnp.left_shift(pick, up) < 0
                    t = jnp.tanh(0.5 * s[r0 : r0 + HALF, b * 128 : (b + 1) * 128])
                    g = t * cl + cl - jnp.where(hit, iv, 0.0)
                    cols = pl.ds(n * WIDE + b * 128, 128)
                    sg[pl.ds((first + i) * HALF, HALF), cols] = g.astype(BF16)

        loop(body)

    def s1_copy(c, d, m, n):
        return remote(
            s1s.at[c, d, m, n], s1r.at[c, d, m, n], s1_ss.at[c, d, m, n], s1_rs.at[c, d, m, n], fast(c, 1 - 2 * d)
        )

    def query_chunk(group, send):
        def body(n):
            out = jnp.dot(sg[rows_of(group), :], w_ref[:, tile_of(n)], preferred_element_type=F32)
            for i, (k, c, j) in enumerate(group):
                low, high = out[i * HALF : i * HALF + QUART], out[i * HALF + QUART : (i + 1) * HALF]
                if k == 0:
                    p0[n, c, j] = out[i * HALF : (i + 1) * HALF]
                if k == 2:
                    s1s[c, 0, 0, n, j] = low.astype(BF16)
                    s1s[c, 1, 0, n, j] = high.astype(BF16)
                if k == 1:
                    p1[n, c, j] = low
                    s1s[c, 0, 1, n, j] = high.astype(BF16)
                if k == 3:
                    p3[n, c, j] = high
                    s1s[c, 1, 1, n, j] = low.astype(BF16)

        loop(body)
        if send is not None:
            for n in range(TILES):
                for c in (0, 1):
                    for d in (0, 1):
                        s1_copy(c, d, send, n).start()

    def weight_tile(n, group):
        return lax.dot_general(
            sg[rows_of(group), tile_of(n)], queries_of(group),
            (((0,), (0,)), ((), ())), preferred_element_type=F32,
        ).reshape(2, RING, 2, 8, dim)

    def x_copy(n):
        rows = pl.ds(2 * n, 2)
        return remote(wg.at[rows, :, 1 - core], xr.at[rows], x_ss.at[n], x_rs.at[n], other)

    def weight_chunk(group):
        def body(n):
            rows = pl.ds(2 * n, 2)
            if group[0] == chunk_a[0]:
                wg[rows] = weight_tile(n, group)
            else:
                wg[rows] = wg[rows] + weight_tile(n, group)
            if group[-1] == chunk_f[-1]:
                x_copy(n).start()

        loop(body)

    score_chunk(chunk_a)
    query_chunk(chunk_a, None)
    for c in (0, 1):
        ag[c, 4, 2].wait_recv()
        ag[c, 4, 3].wait_recv()
        p2a(c, 2)
    for copy in meta_xy:
        copy.wait_recv()
    for d in range(SIDE * SIDE):
        if d >= SIDE and d % SIDE:
            prepare(d)
    for c in (0, 1):
        p2b(c, 0)
    score_chunk(chunk_b)
    query_chunk(chunk_b, None)
    for c in (0, 1):
        p2b(c, 3)
    weight_chunk(chunk_a + chunk_b)
    for c in (0, 1):
        p2b(c, 1)
    score_chunk(chunk_c)
    query_chunk(chunk_c, None)
    for c in (0, 1):
        p2b(c, 2)
    score_chunk(chunk_d)
    query_chunk(chunk_d, 1)
    weight_chunk(chunk_c + chunk_d)
    for j in (0, 3):
        for c in (0, 1):
            ag[c, j, 2].wait_recv()
            ag[c, j, 3].wait_recv()
    score_chunk(chunk_e)
    query_chunk(chunk_e, None)
    for j in (1, 2):
        for c in (0, 1):
            ag[c, j, 2].wait_recv()
            ag[c, j, 3].wait_recv()
    score_chunk(chunk_f)
    weight_chunk(chunk_e + chunk_f)
    query_chunk(chunk_f, 0)

    def z_copy(d, t, n):
        sem = (z_ss.at[d, t, n], z_rs.at[d, t, n], zdev(1 - 2 * d))
        if t == 0:
            return remote(zs.at[d, 2, n, pl.ds(0, 8)], zr.at[d, 2, n, pl.ds(0, 8)], *sem)
        if t < 3:
            return remote(zs.at[d, t - 1, n], zr.at[d, t - 1, n], *sem)
        return remote(zfs.at[d, n], zfr.at[d, n], *sem)

    def piece(r, n):
        i = lax.rem(z + r, RING)
        rows = slice(2 * n, 2 * n + 2)
        return wg[rows, i, core] + xr[rows, i]

    def z_step(d, t, n):
        if t == 0:
            i = lax.rem(z + 4, RING)
            zs[d, 2, n, 0:8] = (wg[2 * n + d, i, core] + xr[2 * n + d, i]).astype(BF16)
        else:
            value = piece(4 - t if d == 0 else 4 + t, n)
            z_copy(d, t - 1, n).wait_recv()
            if t == 1:
                came = zr[d, 2, n, 0:8].astype(F32)
                none = jnp.zeros_like(came)
                value = value + jnp.stack([came, none] if d == 0 else [none, came])
            else:
                value = value + zr[d, t - 2, n].astype(F32).reshape(2, 8, dim)
            value = value.reshape(16, dim)
            if t < 3:
                zs[d, t - 1, n] = value.astype(BF16)
            else:
                zfs[d, n] = value
        go(z_copy(d, t, n))

    def z_hop(t, n):
        z_step(0, t, n)
        z_step(1, t, n)

    def s1_mid(n):
        for c in (0, 1):
            for d, keep in ((0, p1), (1, p3)):
                s1_copy(c, d, 0, n).wait_recv()
                s1s[c, d, 2, n] = (keep[n, c] + s1r[c, d, 0, n].astype(F32)).astype(BF16)
                go(s1_copy(c, d, 2, n))

    def s2_copy(c, d, n):
        return remote(s2s.at[c, d, n], s2r.at[c, d, n], s2_ss.at[c, d, 0, n], s2_rs.at[c, d, 0, n], slow(c, 1 - 2 * d))

    def s3_copy(c, d, n):
        return remote(s3s.at[c, d, n], s3r.at[c, d, n], s2_ss.at[c, d, 1, n], s2_rs.at[c, d, 1, n], slow(c, 1 - 2 * d))

    def s1_end(n):
        for c in (0, 1):
            for d in (0, 1):
                s1_copy(c, d, 1, n).wait_recv()
                s1_copy(c, d, 2, n).wait_recv()
            low = p0[n, c, :, :QUART] + s1r[c, 1, 1, n].astype(F32) + s1r[c, 0, 2, n].astype(F32)
            high = p0[n, c, :, QUART:] + s1r[c, 0, 1, n].astype(F32) + s1r[c, 1, 2, n].astype(F32)
            s2s[c, 0, n, 0] = low[2].astype(BF16)
            s2s[c, 0, n, 1] = high[1].astype(BF16)
            go(s2_copy(c, 0, n))
            s2s[c, 1, n, 0] = high[2].astype(BF16)
            s2s[c, 1, n, 1] = low[3].astype(BF16)
            go(s2_copy(c, 1, n))
            p0[n, c, 0, :QUART] = low[0]
            p0[n, c, 0, QUART:] = high[0]
            p1[n, c, 0] = low[1]
            p3[n, c, 0] = high[3]

    def s2_mid(n):
        for c in (0, 1):
            for d, keep in ((0, p1), (1, p3)):
                s2_copy(c, d, n).wait_recv()
                s3s[c, d, n] = keep[n, c, 0] + s2r[c, d, n, 0].astype(F32)
                go(s3_copy(c, d, n))

    def s2_end(n):
        cols = slice(n * WIDE, (n + 1) * WIDE)
        for c in (0, 1):
            s3_copy(c, 0, n).wait_recv()
            s3_copy(c, 1, n).wait_recv()
            qg_ref[c, :QUART, cols] = p0[n, c, 0, :QUART] + s2r[c, 1, n, 1].astype(F32) + s3r[c, 0, n]
            qg_ref[c, QUART:, cols] = p0[n, c, 0, QUART:] + s2r[c, 0, n, 1].astype(F32) + s3r[c, 1, n]

    @pl.when(odd == 0)
    def _():
        pl.semaphore_wait(met, 2)

    for n in range(TILES):
        x_copy(n).wait_recv()
        z_hop(0, n)
    z_hop(1, 0)
    z_hop(1, 1)
    s1_mid(0)
    z_hop(1, 2)
    z_hop(1, 3)
    s1_mid(1)
    s1_mid(2)
    z_hop(2, 0)
    z_hop(2, 1)
    s1_mid(3)
    z_hop(2, 2)
    z_hop(2, 3)
    s1_end(0)
    s1_end(1)
    z_hop(3, 0)
    s1_end(2)
    z_hop(3, 1)
    s1_end(3)
    s2_mid(0)
    z_hop(3, 2)
    s2_mid(1)
    z_hop(3, 3)
    s2_mid(2)
    s2_mid(3)
    for n in range(TILES):
        s2_end(n)
    for n in range(TILES):
        z_copy(0, 3, n).wait_recv()
        z_copy(1, 3, n).wait_recv()
        wo_ref[2 * n : 2 * n + 2] = piece(0, n) + (zfr[0, n] + zfr[1, n]).reshape(2, 8, dim)
    for n in range(TILES):
        x_copy(n).wait_send()
        for c in (0, 1):
            for d in (0, 1):
                for m in (0, 1):
                    s1_copy(c, d, m, n).wait_send()
    for copy in started:
        copy.wait_send()


def per_device(queries, label_weights, propensity, positives, shortlist, owner_map):
    blocks, block_rows, dim = label_weights.shape
    hbm = pl.BlockSpec(memory_space=pl.ANY)
    vm = pl.BlockSpec(memory_space=pltpu.VMEM)
    dma = pltpu.SemaphoreType.DMA
    qg, wo = pl.pallas_call(
        kernel,
        out_shape=(
            pltpu.VMEM((2, HALF, dim), F32),
            pltpu.VMEM((blocks, 8, dim), F32),
        ),
        in_specs=[hbm] * 6,
        out_specs=(vm, vm),
        scratch_shapes=[
            pltpu.VMEM((SIDE * 2 * SIDE, HALF, dim), BF16),
            pltpu.VMEM((blocks * block_rows, dim), BF16),
            pltpu.VMEM((blocks, block_rows), F32),
            pltpu.VMEM((1, shortlist.shape[1]), I32),
            pltpu.VMEM((1, 128), I32),
            pltpu.VMEM((16, 128), I32),
            pltpu.VMEM((SIDE, SIDE, 16, 128), I32),
            pltpu.VMEM((SIDE * SIDE, 128, 128), I32),
            pltpu.VMEM((SIDE * SIDE, 8, 128), F32),
            pltpu.VMEM((8, 128), F32),
            pltpu.VMEM((SIDE * 2 * SIDE * HALF, blocks * block_rows), BF16),
            pltpu.VMEM((TILES, 2, SIDE, HALF, WIDE), F32),
            pltpu.VMEM((TILES, 2, SIDE, QUART, WIDE), F32),
            pltpu.VMEM((TILES, 2, SIDE, QUART, WIDE), F32),
            pltpu.VMEM((blocks, RING, 2, 8, dim), F32),
            pltpu.VMEM((2, 2, 3, TILES, SIDE, QUART, WIDE), BF16),
            pltpu.VMEM((2, 2, 3, TILES, SIDE, QUART, WIDE), BF16),
            pltpu.VMEM((2, 2, TILES, 2, QUART, WIDE), BF16),
            pltpu.VMEM((2, 2, TILES, 2, QUART, WIDE), BF16),
            pltpu.VMEM((2, 2, TILES, QUART, WIDE), F32),
            pltpu.VMEM((2, 2, TILES, QUART, WIDE), F32),
            pltpu.VMEM((blocks, RING, 8, dim), F32),
            pltpu.VMEM((2, 3, TILES, 16, dim), BF16),
            pltpu.VMEM((2, 3, TILES, 16, dim), BF16),
            pltpu.VMEM((2, TILES, 16, dim), F32),
            pltpu.VMEM((2, TILES, 16, dim), F32),
            dma((7,)),
            dma((3, 4)), dma((3, 4)),
            dma((2, 6, 4)), dma((2, 6, 4)),
            dma((2, 2, 3, TILES)), dma((2, 2, 3, TILES)),
            dma((2, 2, 2, TILES)), dma((2, 2, 2, TILES)),
            dma((TILES,)), dma((TILES,)),
            dma((2, 4, TILES)), dma((2, 4, TILES)),
            pltpu.SemaphoreType.REGULAR,
        ],
        compiler_params=pltpu.CompilerParams(
            collective_id=0, has_side_effects=True, vmem_limit_bytes=66_256_896
        ),
    )(
        queries.reshape(2, HALF, dim),
        label_weights.reshape(blocks * block_rows, dim),
        propensity,
        positives.T,
        shortlist,
        owner_map.reshape(1, -1),
    )
    return qg.reshape(2 * HALF, dim), wo


def solution(mesh):
    in_specs = (
        P(("dp", "label", "section"), None),
        P("label", None, None),
        P("label", None),
        P(("dp", "label", "section"), None),
        P(("dp", "label"), None),
        P(),
    )
    out_specs = (P(("dp", "label", "section"), None), P("label", ("dp", "section"), None))
    return jax.shard_map(
        per_device, mesh=mesh, in_specs=in_specs, out_specs=out_specs, check_vma=False
    )
```
